32 devices in a mesh: grp: 2 (over y), row: 4 (over z), col: 4 (over x, core).
Axes of the slice: x: 2, y: 2, z: 4, core: 2. Of those that a mesh axis runs over, the one named last changes fastest.
Arguments:
- factor: float32 [4, 1024, 1024], P('grp', ('row', 'col')), may hold values from -0.1875 to 0.1875
- pivots: float32 [4, 1024], P('grp', ('row', 'col')), may hold values from 0.5 to 2
- constraints: float32 [4, 1024, 4096], P('grp', None, ('col', 'row')), may hold values from -0.09375 to 0.09375
Outputs:
- q_panels: float32 [4, 1024, 4096], P('row', 'grp', 'col')
The draws below stay inside these ranges and needn't reach their ends.
All inputs are finite; a program needn't handle non-finite values.
Results may differ from the reference program's by a relative error of at most 0.0011.
Values may be sent and summed in bfloat16 or wider, within the bound.
A program may use at most 64 MiB of HBM per device.

```python
import math
import jax
import jax.numpy as jnp
from jax import lax

M = 1024
N = 4096
NBLK = 4
STRIP = 256
N_ROW = 4
N_COL = 4


def steps_of(own_key, extent, shards, low, top_value):
    factor_of = 1.0
    for axis_at, blocks in shards:
        draws = jax.random.uniform(jax.random.fold_in(jax.random.fold_in(own_key, 6), axis_at), (blocks,), jnp.float32, low / len(shards), top_value / len(shards))
        factor_of = factor_of * jnp.repeat(jnp.exp(draws), extent[axis_at] // blocks).reshape((-1,) + (1,) * (len(extent) - 1 - axis_at))
    return factor_of


def gaussian(own_key, shape, scale, reach, pieces=(), held_as=jnp.bfloat16):
    drawn = scale * jax.random.normal(own_key, shape, jnp.float32)
    if pieces:
        drawn = drawn * steps_of(own_key, shape, pieces, -0.22, 0.18)
    return jnp.clip(drawn, -reach, reach).astype(held_as)


def setup_inputs(seed: int = 0) -> dict:
    keys = jax.random.split(jax.random.key(seed), 4)
    return {
        "factor": gaussian(keys[0], (NBLK, M, M), (1.0 / M ** 0.5), 0.1875, ((0, 2), (1, 16)), jnp.float32),
        "pivots": jnp.clip(jnp.exp(math.log(2.0) - 1.3862944 * jax.random.uniform(keys[1], (NBLK, M), jnp.float32) ** steps_of(keys[1], (NBLK, M), ((0, 2), (1, 16)), -0.2, 0.2)), 0.5, 2.0),
        "constraints": gaussian(keys[2], (NBLK, M, N), (1.0 / (M * NBLK) ** 0.5), 0.09375, ((0, 2), (2, 16)), jnp.float32),
    }


def reference(factor, pivots, constraints):
    positions = jnp.arange(M, dtype=jnp.int32)
    strict_lower = positions[None, :] < positions[:, None]

    def one_block(running, block_items):
        factor_rows, pivot_rows, right_side = block_items
        triangle = jnp.where(strict_lower, factor_rows, jnp.zeros_like(factor_rows)) + jnp.diag(pivot_rows)
        projected = jnp.dot(triangle, right_side, precision=lax.Precision.HIGHEST, preferred_element_type=jnp.float32).astype(jnp.bfloat16)
        product = lax.dot_general(projected, projected, (((0,), (0,)), ((), ())), preferred_element_type=jnp.float32)
        return running + product, None

    running, leftover = lax.scan(one_block, jnp.zeros((N, N), jnp.float32), (factor, pivots, constraints))
    regrouped = running.reshape(N_COL, N_ROW, STRIP, N).transpose(1, 0, 2, 3)
    return regrouped.reshape(N_ROW, N // N_ROW, N)
```

```python
import functools
import jax
import jax.numpy as jnp
from jax import lax
from jax.experimental import pallas as pl
from jax.experimental.pallas import tpu as pltpu
from jax.sharding import PartitionSpec as P

MESH = pl.DeviceIdType.MESH
f32 = jnp.float32
bf16 = jnp.bfloat16
W = 256


def kernel(G, nb, tin, c_hbm, out, tbuf, cbuf, chi, clo, acc, colbuf, rowt, sbuf, rbuf,
           csem, tss, trs, pzs, pzr, pxs, pxr, rss, rsr):
    g, z, c = lax.axis_index("grp"), lax.axis_index("row"), lax.axis_index("col")
    sib = c + 1 - 2 * (c % 2)
    xn = (c + 2) % 4
    d_up, d_dn = (g, z + 1, c), (g, z - 1, c)
    d_xn, d_sib = (g, z, xn), (g, z, sib)
    d_y = (1 - g, z, c)
    piece = tin.shape[2]

    def order(zz, j):
        if j == 0:
            return zz
        if j == 1:
            return zz - 1 + 2 * ((3 - zz) // 3)
        if j == 2:
            return zz + 1 + (3 - zz) // 3 - 3 * (zz // 3)
        return 3 - 3 * (zz // 2)

    cload = pltpu.make_async_copy(c_hbm, cbuf, csem)
    cload.start()

    bar = pltpu.get_barrier_semaphore()

    def hello(dev):
        pl.semaphore_signal(bar, inc=1, device_id=dev, device_id_type=MESH)

    hello(d_xn)
    hello(d_sib)
    if G == 2:
        hello(d_y)

    @pl.when(z < 3)
    def _():
        hello(d_up)

    @pl.when(z > 0)
    def _():
        hello(d_dn)

    for kc in range(4):
        @pl.when(kc <= z)
        def _():
            tbuf[kc, :, pl.ds(pl.multiple_of(W * z + piece * c, piece), piece), :] = tin[kc]

    pl.semaphore_wait(bar, (3 if G == 2 else 2) + (z + 3) // 4 + 1 - z // 3)

    def remote(ref, ss, rs, dev):
        return pltpu.make_async_remote_copy(
            src_ref=ref, dst_ref=ref, send_sem=ss, recv_sem=rs, device_id=dev, device_id_type=MESH)

    def tcopy(route, arrive, r, kc, col, dev):
        ref = tbuf.at[kc, :, pl.ds(pl.multiple_of(W * r + piece * col, piece), piece), :]
        return remote(ref, tss.at[route, r, kc], trs.at[arrive, r, kc], dev)

    def t_up(r, kc):
        return tcopy(0, 0, r, kc, c, d_up)

    def t_dn(r, kc):
        return tcopy(1, 0, r, kc, c, d_dn)

    def t_xn(r, kc):
        return tcopy(2, 1, r, kc, c, d_xn)

    def t_sib(r, kc):
        return tcopy(3, 2, r, kc, c, d_sib)

    def t_fwd(r, kc):
        return tcopy(4, 3, r, kc, xn, d_sib)

    def t_first(j):
        r = order(z, j)

        @pl.loop(0, r + 1)
        def _(kc):
            if j > 0:
                t_up(r, kc).wait_recv()

            @pl.when((r <= z) & (z < 3))
            def _():
                t_up(r, kc).start()

            @pl.when((r >= z) & (z > 0))
            def _():
                t_dn(r, kc).start()

            t_xn(r, kc).start()
            t_sib(r, kc).start()

    def t_second(j):
        r = order(z, j)

        @pl.loop(0, r + 1)
        def _(kc):
            t_xn(r, kc).wait_recv()
            t_fwd(r, kc).start()

    def pz(s, rg, up):
        return remote(colbuf.at[s, rg], pzs.at[0 if up else 1, s, rg], pzr.at[s, rg], d_up if up else d_dn)

    def px(route, col, rg):
        return remote(rowt.at[col, rg], pxs.at[route, rg], pxr.at[route, rg], d_xn if route == 0 else d_sib)

    def project(j):
        r = order(z, j)

        @pl.loop(0, r + 1)
        def _(kc):
            t_sib(r, kc).wait_recv()
            t_fwd(r, kc).wait_recv()

        rows = pl.ds(pl.multiple_of(W * r, W), W)
        for b in range(nb):
            acc[...] = jnp.zeros_like(acc)

            @pl.loop(0, r + 1)
            def _(kc):
                t = tbuf[kc, b, rows, :]
                th = t.astype(bf16)
                tl = (t - th.astype(f32)).astype(bf16)
                ks = pl.ds(pl.multiple_of(W * kc, W), W)
                ch = chi[b, ks, :]
                acc[...] += (jnp.dot(th, ch, preferred_element_type=f32)
                             + jnp.dot(th, clo[b, ks, :], preferred_element_type=f32)
                             + jnp.dot(tl, ch, preferred_element_type=f32))

            full = acc[...]
            colbuf[z, r, W * b:W * (b + 1), :] = full.astype(bf16)
            rowt[c, r, :, W * b:W * (b + 1)] = full.T.astype(bf16)

        @pl.when(z < 3)
        def _():
            pz(z, r, True).start()

        @pl.when(z > 0)
        def _():
            pz(z, r, False).start()

        px(0, c, r).start()
        px(1, c, r).start()

    t_first(0)
    cload.wait()
    for b in range(nb):
        cc = cbuf[b]
        hi = cc.astype(bf16)
        chi[b] = hi
        clo[b] = (cc - hi.astype(f32)).astype(bf16)
    for j in range(1, 4):
        t_first(j)
        t_second(j - 1)
        project(j - 1)
    t_second(3)
    project(3)

    def block(cp, s):
        total = jnp.dot(rowt[cp, 0], colbuf[s, 0], preferred_element_type=f32)
        for rg in range(1, 4):
            total += jnp.dot(rowt[cp, rg], colbuf[s, rg], preferred_element_type=f32)
        return total

    def rs(s):
        return pltpu.make_async_remote_copy(
            src_ref=sbuf.at[s], dst_ref=rbuf.at[s], send_sem=rss.at[s], recv_sem=rsr.at[s],
            device_id=d_y, device_id_type=MESH)

    def gram(s):
        cols = pl.ds(pl.multiple_of(W * s, W), W)
        if G == 2:
            @pl.loop(0, 2)
            def _(i):
                sbuf[s, pl.ds(pl.multiple_of(W * i, W), W), :] = block(2 * (1 - g) + i, s)

            rs(s).start()

            @pl.loop(0, 2)
            def _(i):
                out[pl.ds(pl.multiple_of(W * i, W), W), cols] = block(2 * g + i, s)
        else:
            @pl.loop(0, 4)
            def _(i):
                out[pl.ds(pl.multiple_of(W * i, W), W), cols] = block(i, s)

    def z_arrivals(d, i):
        lo, hi = z - d, z + d

        @pl.when(lo >= 0)
        def _():
            rg = order(lo, i)
            pz(lo, rg, True).wait_recv()

            @pl.when(z < 3)
            def _():
                pz(lo, rg, True).start()

        @pl.when(hi <= 3)
        def _():
            rg = order(hi, i)
            pz(hi, rg, False).wait_recv()

            @pl.when(z > 0)
            def _():
                pz(hi, rg, False).start()

    for i in range(4):
        r = order(z, i)
        px(0, c, r).wait_recv()
        px(2, xn, r).start()
        z_arrivals(1, i)
    for i in range(4):
        px(1, c, i).wait_recv()
        px(2, c, i).wait_recv()
    gram(z)
    for d in (1, 2, 3):
        if d > 1:
            for i in range(4):
                z_arrivals(d, i)

        @pl.when(z - d >= 0)
        def _():
            gram(z - d)

        @pl.when(z + d <= 3)
        def _():
            gram(z + d)

    if G == 2:
        def finish(s):
            cols = pl.ds(pl.multiple_of(W * s, W), W)
            rs(s).wait_recv()
            out[:, cols] = out[:, cols] + rbuf[s]

        finish(z)
        for d in (1, 2, 3):
            @pl.when(z - d >= 0)
            def _():
                finish(z - d)

            @pl.when(z + d <= 3)
            def _():
                finish(z + d)

    for r in range(4):
        for kc in range(r + 1):
            @pl.when((r <= z) & (z < 3))
            def _():
                t_up(r, kc).wait_send()

            @pl.when((r >= z) & (z > 0))
            def _():
                t_dn(r, kc).wait_send()

            t_xn(r, kc).wait_send()
            t_sib(r, kc).wait_send()
            t_fwd(r, kc).wait_send()
        for s in range(4):
            @pl.when((s <= z) & (z < 3))
            def _():
                pz(s, r, True).wait_send()

            @pl.when((s >= z) & (z > 0))
            def _():
                pz(s, r, False).wait_send()

        px(0, c, r).wait_send()
        px(1, c, r).wait_send()
        px(2, xn, r).wait_send()
        if G == 2:
            rs(r).wait_send()


def body(G, factor, pivots, constraints):
    nb, piece, order_m = factor.shape
    strip = constraints.shape[2]
    assert strip == W and order_m == 4 * W and piece * 4 == W
    first = (lax.axis_index("row") * 4 + lax.axis_index("col")) * piece
    row_ids = first + lax.broadcasted_iota(jnp.int32, factor.shape, 1)
    col_ids = lax.broadcasted_iota(jnp.int32, factor.shape, 2)
    tri = jnp.where(col_ids < row_ids, factor, jnp.where(col_ids == row_ids, pivots[:, :, None], 0.0))
    tin = tri.reshape(nb, piece, 4, W).transpose(2, 0, 1, 3)
    rows_out = 2 * W if G == 2 else 4 * W
    dma = pltpu.SemaphoreType.DMA
    half = (4, 2 * W, W) if G == 2 else (1, 8, 128)
    result = pl.pallas_call(
        functools.partial(kernel, G, nb),
        out_shape=jax.ShapeDtypeStruct((rows_out, 4 * W), f32),
        in_specs=[pl.BlockSpec(memory_space=pltpu.VMEM), pl.BlockSpec(memory_space=pl.ANY)],
        out_specs=pl.BlockSpec(memory_space=pltpu.VMEM),
        scratch_shapes=[
            pltpu.VMEM((4, nb, 4 * W, W), f32),
            pltpu.VMEM((nb, 4 * W, W), f32),
            pltpu.VMEM((nb, 4 * W, W), bf16),
            pltpu.VMEM((nb, 4 * W, W), bf16),
            pltpu.VMEM((W, W), f32),
            pltpu.VMEM((4, 4, nb * W, W), bf16),
            pltpu.VMEM((4, 4, W, nb * W), bf16),
            pltpu.VMEM(half, f32),
            pltpu.VMEM(half, f32),
            dma,
            dma((5, 4, 4)),
            dma((4, 4, 4)),
            dma((2, 4, 4)),
            dma((4, 4)),
            dma((3, 4)),
            dma((3, 4)),
            dma((4,)),
            dma((4,)),
        ],
        compiler_params=pltpu.CompilerParams(
            collective_id=0, has_side_effects=True, vmem_limit_bytes=52 << 20),
    )(tin, constraints)
    if G != 2:
        result = lax.psum_scatter(result, "grp", scatter_dimension=0, tiled=True)
    return result[None]


def solution(mesh):
    in_specs = (
        P("grp", ("row", "col"), None),
        P("grp", ("row", "col")),
        P("grp", None, ("col", "row")),
    )
    return jax.shard_map(
        functools.partial(body, mesh.shape["grp"]), mesh=mesh, in_specs=in_specs,
        out_specs=P("row", "grp", "col"), check_vma=False)
```

```python
import functools
import jax
import jax.numpy as jnp
from jax import lax
from jax.experimental import pallas as pl
from jax.experimental.pallas import tpu as pltpu
from jax.sharding import PartitionSpec as P

MESH = pl.DeviceIdType.MESH
f32 = jnp.float32
bf16 = jnp.bfloat16
W = 256


def kernel(G, nb, fac, piv, c_hbm, out, tbuf, cbuf, chi, clo, acc, colbuf, rowt, obuf, sbuf, rbuf,
           csem, tss, trs, pzs, pzr, phs, phr, pxs, pxr, rss, rsr, osem):
    g, z, c = lax.axis_index("grp"), lax.axis_index("row"), lax.axis_index("col")
    sib = c + 1 - 2 * (c % 2)
    xn = (c + 2) % 4
    d_up, d_dn = (g, z + 1, c), (g, z - 1, c)
    d_xn, d_sib = (g, z, xn), (g, z, sib)
    d_y = (1 - g, z, c)
    piece = fac.shape[1]

    def order(zz, j):
        if j == 0:
            return zz
        if j == 1:
            return zz - 1 + 2 * ((3 - zz) // 3)
        if j == 2:
            return zz + 1 + (3 - zz) // 3 - 3 * (zz // 3)
        return 3 - 3 * (zz // 2)

    cload = pltpu.make_async_copy(c_hbm, cbuf, csem)
    cload.start()

    bar = pltpu.get_barrier_semaphore()

    def hello(dev):
        pl.semaphore_signal(bar, inc=1, device_id=dev, device_id_type=MESH)

    hello(d_xn)
    hello(d_sib)
    if G == 2:
        hello(d_y)

    @pl.when(z < 3)
    def _():
        hello(d_up)

    @pl.when(z > 0)
    def _():
        hello(d_dn)

    for kc in range(4):
        @pl.when(kc <= z)
        def _():
            start = W * z + piece * c
            rows = start + lax.broadcasted_iota(jnp.int32, (piece, W), 0)
            cols = W * kc + lax.broadcasted_iota(jnp.int32, (piece, W), 1)
            for b in range(nb):
                diag = jnp.where(cols == rows, jnp.broadcast_to(piv[b:b + 1, :], (piece, W)), 0.0)
                tbuf[kc, b, pl.ds(pl.multiple_of(start, piece), piece), :] = jnp.where(
                    cols < rows, fac[b, :, W * kc:W * (kc + 1)], diag)

    pl.semaphore_wait(bar, (3 if G == 2 else 2) + (z + 3) // 4 + 1 - z // 3)

    def remote(ref, ss, rs, dev):
        return pltpu.make_async_remote_copy(
            src_ref=ref, dst_ref=ref, send_sem=ss, recv_sem=rs, device_id=dev, device_id_type=MESH)

    def tcopy(route, arrive, r, kc, col, dev):
        ref = tbuf.at[kc, :, pl.ds(pl.multiple_of(W * r + piece * col, piece), piece), :]
        return remote(ref, tss.at[route, r, kc], trs.at[arrive, r, kc], dev)

    def t_up(r, kc):
        return tcopy(0, 0, r, kc, c, d_up)

    def t_dn(r, kc):
        return tcopy(1, 0, r, kc, c, d_dn)

    def t_xn(r, kc):
        return tcopy(2, 1, r, kc, c, d_xn)

    def t_sib(r, kc):
        return tcopy(3, 2, r, kc, c, d_sib)

    def t_fwd(r, kc):
        return tcopy(4, 3, r, kc, xn, d_sib)

    def t_first(j):
        r = order(z, j)

        @pl.loop(0, r + 1)
        def _(kc):
            if j > 0:
                t_up(r, kc).wait_recv()

            @pl.when((r <= z) & (z < 3))
            def _():
                t_up(r, kc).start()

            @pl.when((r >= z) & (z > 0))
            def _():
                t_dn(r, kc).start()

            t_xn(r, kc).start()
            t_sib(r, kc).start()

    def t_second(j):
        r = order(z, j)

        @pl.loop(0, r + 1)
        def _(kc):
            t_xn(r, kc).wait_recv()
            t_fwd(r, kc).start()

    def pz(s, rg, up):
        return remote(colbuf.at[s, rg], pzs.at[0 if up else 1, s, rg], pzr.at[s, rg], d_up if up else d_dn)

    def px(route, col, rg):
        return remote(rowt.at[col, rg], pxs.at[route, rg], pxr.at[route, rg], d_xn if route == 0 else d_sib)

    def project(j):
        r = order(z, j)

        @pl.loop(0, r + 1)
        def _(kc):
            t_sib(r, kc).wait_recv()
            t_fwd(r, kc).wait_recv()

        rows = pl.ds(pl.multiple_of(W * r, W), W)
        for b in range(nb):
            acc[...] = jnp.zeros_like(acc)

            @pl.loop(0, r + 1)
            def _(kc):
                t = tbuf[kc, b, rows, :]
                th = t.astype(bf16)
                tl = (t - th.astype(f32)).astype(bf16)
                ks = pl.ds(pl.multiple_of(W * kc, W), W)
                ch = chi[b, ks, :]
                acc[...] += (jnp.dot(th, ch, preferred_element_type=f32)
                             + jnp.dot(th, clo[b, ks, :], preferred_element_type=f32)
                             + jnp.dot(tl, ch, preferred_element_type=f32))

            full = acc[...]
            colbuf[z, r, W * b:W * (b + 1), :] = full.astype(bf16)
            rowt[c, r, :, W * b:W * (b + 1)] = full.T.astype(bf16)

        @pl.when(z < 3)
        def _():
            pz(z, r, True).start()

        @pl.when(z > 0)
        def _():
            pz(z, r, False).start()

        px(0, c, r).start()
        px(1, c, r).start()

    t_first(0)
    cload.wait()
    for b in range(nb):
        cc = cbuf[b]
        hi = cc.astype(bf16)
        chi[b] = hi
        clo[b] = (cc - hi.astype(f32)).astype(bf16)
    t_first(1)
    t_first(2)
    t_second(0)
    project(0)
    t_second(1)
    project(1)
    t_first(3)
    t_second(2)
    project(2)
    t_second(3)
    project(3)

    H = W // 2

    def block(cp, s, lo, n):
        total = jnp.dot(rowt[cp, 0], colbuf[s, 0, :, lo:lo + n], preferred_element_type=f32)
        for rg in range(1, 4):
            total += jnp.dot(rowt[cp, rg], colbuf[s, rg, :, lo:lo + n], preferred_element_type=f32)
        return total

    def rs(s, h):
        return pltpu.make_async_remote_copy(
            src_ref=sbuf.at[s, h], dst_ref=rbuf.at[s, h], send_sem=rss.at[s, h], recv_sem=rsr.at[s, h],
            device_id=d_y, device_id_type=MESH)

    def emit(s, h):
        cols = pl.ds(pl.multiple_of(W * s + H * h, H), H)
        return pltpu.make_async_copy(obuf.at[:, cols], out.at[:, cols], osem.at[s, h])

    def gram(s, halves):
        lo, n = H * halves[0], H * len(halves)
        cols = pl.ds(pl.multiple_of(W * s + lo, H), n)
        if G == 2:
            @pl.loop(0, 2)
            def _(i):
                rows = pl.ds(pl.multiple_of(W * i, W), W)
                t = block(2 * (1 - g) + i, s, lo, n)
                for k, h in enumerate(halves):
                    sbuf[s, h, rows, :] = t[:, H * k:H * (k + 1)]

            for h in halves:
                rs(s, h).start()

            @pl.loop(0, 2)
            def _(i):
                obuf[pl.ds(pl.multiple_of(W * i, W), W), cols] = block(2 * g + i, s, lo, n)
        else:
            @pl.loop(0, 4)
            def _(i):
                obuf[pl.ds(pl.multiple_of(W * i, W), W), cols] = block(i, s, lo, n)

    def finish(s):
        for h in (0, 1):
            if G == 2:
                cols = pl.ds(pl.multiple_of(W * s + H * h, H), H)
                rs(s, h).wait_recv()
                obuf[:, cols] = obuf[:, cols] + rbuf[s, h]
            emit(s, h).start()

    def ph(s, rg, h, up):
        return remote(colbuf.at[s, rg, :, H * h:H * (h + 1)], phs.at[rg, h], phr.at[rg, h], d_up if up else d_dn)

    def near(i):
        lo, hi = z - 1, z + 1

        @pl.when(lo >= 0)
        def _():
            rg = order(lo, i)
            pz(lo, rg, True).wait_recv()

            @pl.when(z < 3)
            def _():
                pz(lo, rg, True).start()

        @pl.when(hi <= 3)
        def _():
            rg = order(hi, i)
            pz(hi, rg, False).wait_recv()

            @pl.when(z > 0)
            def _():
                pz(hi, rg, False).start()

    def second(s, up):
        for i in range(4):
            pz(s, order(s, i), up).wait_recv()

        @pl.when((z == 1) | (z == 2))
        def _():
            for h in (0, 1):
                for rg in range(4):
                    ph(s, rg, h, up).start()

        gram(s, (0, 1))

    def third(s, up):
        for h in (0, 1):
            for rg in range(4):
                ph(s, rg, h, up).wait_recv()
            gram(s, (h,))

    def each(d, fn):
        @pl.when(z - d >= 0)
        def _():
            fn(z - d, True)

        @pl.when(z + d <= 3)
        def _():
            fn(z + d, False)

    for i in range(4):
        near(i)
        r = order(z, i)
        px(0, c, r).wait_recv()
        px(2, xn, r).start()
    for i in range(4):
        px(1, c, i).wait_recv()
        px(2, c, i).wait_recv()
    gram(z, (0, 1))
    each(1, lambda s, up: gram(s, (0, 1)))
    each(2, second)
    finish(z)
    each(1, lambda s, up: finish(s))
    each(2, lambda s, up: finish(s))
    each(3, third)
    each(3, lambda s, up: finish(s))

    for r in range(4):
        for kc in range(r + 1):
            @pl.when((r <= z) & (z < 3))
            def _():
                t_up(r, kc).wait_send()

            @pl.when((r >= z) & (z > 0))
            def _():
                t_dn(r, kc).wait_send()

            t_xn(r, kc).wait_send()
            t_sib(r, kc).wait_send()
            t_fwd(r, kc).wait_send()
        for s in range(4):
            @pl.when((s <= z) & (z < 3) & (z - s < 2))
            def _():
                pz(s, r, True).wait_send()

            @pl.when((s >= z) & (z > 0) & (s - z < 2))
            def _():
                pz(s, r, False).wait_send()

        px(0, c, r).wait_send()
        px(1, c, r).wait_send()
        px(2, xn, r).wait_send()
        for h in (0, 1):
            @pl.when((z == 1) | (z == 2))
            def _():
                ph(3, r, h, False).wait_send()

            if G == 2:
                rs(r, h).wait_send()
            emit(r, h).wait()


def body(G, factor, pivots, constraints):
    nb, piece, order_m = factor.shape
    strip = constraints.shape[2]
    assert strip == W and order_m == 4 * W and piece * 4 == W
    rows_out = 2 * W if G == 2 else 4 * W
    dma = pltpu.SemaphoreType.DMA
    half = (4, 2, 2 * W, W // 2) if G == 2 else (1, 1, 8, 128)
    result = pl.pallas_call(
        functools.partial(kernel, G, nb),
        out_shape=jax.ShapeDtypeStruct((rows_out, 4 * W), f32),
        in_specs=[
            pl.BlockSpec(memory_space=pltpu.VMEM),
            pl.BlockSpec(memory_space=pltpu.VMEM),
            pl.BlockSpec(memory_space=pl.ANY),
        ],
        out_specs=pl.BlockSpec(memory_space=pl.ANY),
        scratch_shapes=[
            pltpu.VMEM((4, nb, 4 * W, W), f32),
            pltpu.VMEM((nb, 4 * W, W), f32),
            pltpu.VMEM((nb, 4 * W, W), bf16),
            pltpu.VMEM((nb, 4 * W, W), bf16),
            pltpu.VMEM((W, W), f32),
            pltpu.VMEM((4, 4, nb * W, W), bf16),
            pltpu.VMEM((4, 4, W, nb * W), bf16),
            pltpu.VMEM((rows_out, 4 * W), f32),
            pltpu.VMEM(half, f32),
            pltpu.VMEM(half, f32),
            dma,
            dma((5, 4, 4)),
            dma((4, 4, 4)),
            dma((2, 4, 4)),
            dma((4, 4)),
            dma((4, 2)),
            dma((4, 2)),
            dma((3, 4)),
            dma((3, 4)),
            dma((4, 2)),
            dma((4, 2)),
            dma((4, 2)),
        ],
        compiler_params=pltpu.CompilerParams(
            collective_id=0, has_side_effects=True, vmem_limit_bytes=52 << 20),
    )(factor, jnp.tile(pivots, (1, 4)), constraints)
    if G != 2:
        result = lax.psum_scatter(result, "grp", scatter_dimension=0, tiled=True)
    return result[None]


def solution(mesh):
    in_specs = (
        P("grp", ("row", "col"), None),
        P("grp", ("row", "col")),
        P("grp", None, ("col", "row")),
    )
    return jax.shard_map(
        functools.partial(body, mesh.shape["grp"]), mesh=mesh, in_specs=in_specs,
        out_specs=P("row", "grp", "col"), check_vma=False)
```

```python
import functools
import jax
import jax.numpy as jnp
from jax import lax
from jax.experimental import pallas as pl
from jax.experimental.pallas import tpu as pltpu
from jax.sharding import PartitionSpec as P

MESH = pl.DeviceIdType.MESH
f32 = jnp.float32
bf16 = jnp.bfloat16
W = 256


def kernel(G, nb, fac, piv, c_hbm, out, tbuf, cbuf, chi, clo, acc, colbuf, rowt, obuf, sbuf, rbuf,
           csem, tss, trs, pzs, pzr, phs, phr, pxs, pxr, rss, rsr, osem):
    g, z, c = lax.axis_index("grp"), lax.axis_index("row"), lax.axis_index("col")
    sib = c + 1 - 2 * (c % 2)
    xn = (c + 2) % 4
    d_up, d_dn = (g, z + 1, c), (g, z - 1, c)
    d_xn, d_sib = (g, z, xn), (g, z, sib)
    d_y = (1 - g, z, c)
    piece = fac.shape[1]

    def order(zz, j):
        if j == 0:
            return zz
        if j == 1:
            return zz - 1 + 2 * ((3 - zz) // 3)
        if j == 2:
            return zz + 1 + (3 - zz) // 3 - 3 * (zz // 3)
        return 3 - 3 * (zz // 2)

    cload = pltpu.make_async_copy(c_hbm, cbuf, csem)
    cload.start()

    bar = pltpu.get_barrier_semaphore()

    def hello(dev):
        pl.semaphore_signal(bar, inc=1, device_id=dev, device_id_type=MESH)

    hello(d_xn)
    hello(d_sib)
    if G == 2:
        hello(d_y)

    @pl.when(z < 3)
    def _():
        hello(d_up)

    @pl.when(z > 0)
    def _():
        hello(d_dn)

    for kc in range(4):
        @pl.when(kc <= z)
        def _():
            start = W * z + piece * c
            rows = start + lax.broadcasted_iota(jnp.int32, (piece, W), 0)
            cols = W * kc + lax.broadcasted_iota(jnp.int32, (piece, W), 1)
            for b in range(nb):
                diag = jnp.where(cols == rows, jnp.broadcast_to(piv[b:b + 1, :], (piece, W)), 0.0)
                tbuf[kc, b, pl.ds(pl.multiple_of(start, piece), piece), :] = jnp.where(
                    cols < rows, fac[b, :, W * kc:W * (kc + 1)], diag)

    pl.semaphore_wait(bar, (3 if G == 2 else 2) + (z + 3) // 4 + 1 - z // 3)

    def remote(ref, ss, rs, dev):
        return pltpu.make_async_remote_copy(
            src_ref=ref, dst_ref=ref, send_sem=ss, recv_sem=rs, device_id=dev, device_id_type=MESH)

    def tcopy(route, arrive, r, kc, col, dev):
        ref = tbuf.at[kc, :, pl.ds(pl.multiple_of(W * r + piece * col, piece), piece), :]
        return remote(ref, tss.at[route, r, kc], trs.at[arrive, r, kc], dev)

    def t_up(r, kc):
        return tcopy(0, 0, r, kc, c, d_up)

    def t_dn(r, kc):
        return tcopy(1, 0, r, kc, c, d_dn)

    def t_xn(r, kc):
        return tcopy(2, 1, r, kc, c, d_xn)

    def t_sib(r, kc):
        return tcopy(3, 2, r, kc, c, d_sib)

    def t_fwd(r, kc):
        return tcopy(4, 3, r, kc, xn, d_sib)

    def t_first(j):
        r = order(z, j)

        @pl.loop(0, r + 1)
        def _(kc):
            if j > 0:
                t_up(r, kc).wait_recv()

            @pl.when((r <= z) & (z < 3))
            def _():
                t_up(r, kc).start()

            @pl.when((r >= z) & (z > 0))
            def _():
                t_dn(r, kc).start()

            t_xn(r, kc).start()
            t_sib(r, kc).start()

    def t_second(j):
        r = order(z, j)

        @pl.loop(0, r + 1)
        def _(kc):
            t_xn(r, kc).wait_recv()
            t_fwd(r, kc).start()

    def pz(s, rg, up):
        return remote(colbuf.at[s, rg], pzs.at[0 if up else 1, s, rg], pzr.at[s, rg], d_up if up else d_dn)

    def px(route, col, rg):
        return remote(rowt.at[col, rg], pxs.at[route, rg], pxr.at[route, rg], d_xn if route == 0 else d_sib)

    def project(j):
        r = order(z, j)

        @pl.loop(0, r + 1)
        def _(kc):
            t_sib(r, kc).wait_recv()
            t_fwd(r, kc).wait_recv()

        rows = pl.ds(pl.multiple_of(W * r, W), W)
        for b in range(nb):
            acc[...] = jnp.zeros_like(acc)

            @pl.loop(0, r + 1)
            def _(kc):
                t = tbuf[kc, b, rows, :]
                th = t.astype(bf16)
                tl = (t - th.astype(f32)).astype(bf16)
                ks = pl.ds(pl.multiple_of(W * kc, W), W)
                ch = chi[b, ks, :]
                acc[...] += (jnp.dot(th, ch, preferred_element_type=f32)
                             + jnp.dot(th, clo[b, ks, :], preferred_element_type=f32)
                             + jnp.dot(tl, ch, preferred_element_type=f32))

            full = acc[...]
            colbuf[z, r, W * b:W * (b + 1), :] = full.astype(bf16)
            rowt[c, r, :, W * b:W * (b + 1)] = full.T.astype(bf16)

        @pl.when(z < 3)
        def _():
            pz(z, r, True).start()

        @pl.when(z > 0)
        def _():
            pz(z, r, False).start()

        px(0, c, r).start()
        px(1, c, r).start()

    t_first(0)
    cload.wait()
    for b in range(nb):
        cc = cbuf[b]
        hi = cc.astype(bf16)
        chi[b] = hi
        clo[b] = (cc - hi.astype(f32)).astype(bf16)
    t_first(1)
    t_first(2)
    t_second(0)
    project(0)
    t_first(3)
    t_second(1)
    project(1)
    t_second(2)
    project(2)
    t_second(3)
    project(3)

    H = W // 2

    def block(cp, s, lo, n):
        total = jnp.dot(rowt[cp, 0], colbuf[s, 0, :, lo:lo + n], preferred_element_type=f32)
        for rg in range(1, 4):
            total += jnp.dot(rowt[cp, rg], colbuf[s, rg, :, lo:lo + n], preferred_element_type=f32)
        return total

    def rs(s, h):
        return pltpu.make_async_remote_copy(
            src_ref=sbuf.at[s, h], dst_ref=rbuf.at[s, h], send_sem=rss.at[s, h], recv_sem=rsr.at[s, h],
            device_id=d_y, device_id_type=MESH)

    def emit(s, h):
        cols = pl.ds(pl.multiple_of(W * s + H * h, H), H)
        return pltpu.make_async_copy(obuf.at[:, cols], out.at[:, cols], osem.at[s, h])

    def gram(s, halves):
        lo, n = H * halves[0], H * len(halves)
        cols = pl.ds(pl.multiple_of(W * s + lo, H), n)
        if G == 2:
            @pl.loop(0, 2)
            def _(i):
                rows = pl.ds(pl.multiple_of(W * i, W), W)
                t = block(2 * (1 - g) + i, s, lo, n)
                for k, h in enumerate(halves):
                    sbuf[s, h, rows, :] = t[:, H * k:H * (k + 1)]

            for h in halves:
                rs(s, h).start()

            @pl.loop(0, 2)
            def _(i):
                obuf[pl.ds(pl.multiple_of(W * i, W), W), cols] = block(2 * g + i, s, lo, n)
        else:
            @pl.loop(0, 4)
            def _(i):
                obuf[pl.ds(pl.multiple_of(W * i, W), W), cols] = block(i, s, lo, n)

    def finish(s):
        for h in (0, 1):
            if G == 2:
                cols = pl.ds(pl.multiple_of(W * s + H * h, H), H)
                rs(s, h).wait_recv()
                obuf[:, cols] = obuf[:, cols] + rbuf[s, h]
            emit(s, h).start()

    def ph(s, rg, h, up):
        return remote(colbuf.at[s, rg, :, H * h:H * (h + 1)], phs.at[rg, h], phr.at[rg, h], d_up if up else d_dn)

    def near(i):
        lo, hi = z - 1, z + 1

        @pl.when(lo >= 0)
        def _():
            rg = order(lo, i)
            pz(lo, rg, True).wait_recv()

            @pl.when(z < 3)
            def _():
                pz(lo, rg, True).start()

        @pl.when(hi <= 3)
        def _():
            rg = order(hi, i)
            pz(hi, rg, False).wait_recv()

            @pl.when(z > 0)
            def _():
                pz(hi, rg, False).start()

    def second(s, up):
        for i in range(4):
            pz(s, order(s, i), up).wait_recv()

        @pl.when((z == 1) | (z == 2))
        def _():
            for h in (0, 1):
                for rg in range(4):
                    ph(s, rg, h, up).start()

        gram(s, (0, 1))

    def third(s, up):
        for h in (0, 1):
            for rg in range(4):
                ph(s, rg, h, up).wait_recv()
            gram(s, (h,))

    def each(d, fn):
        @pl.when(z - d >= 0)
        def _():
            fn(z - d, True)

        @pl.when(z + d <= 3)
        def _():
            fn(z + d, False)

    for i in range(4):
        near(i)
        r = order(z, i)
        px(0, c, r).wait_recv()
        px(2, xn, r).start()
    for i in range(4):
        px(1, c, i).wait_recv()
        px(2, c, i).wait_recv()
    gram(z, (0, 1))
    each(1, lambda s, up: gram(s, (0, 1)))
    each(2, second)
    finish(z)
    each(1, lambda s, up: finish(s))
    each(3, third)
    each(2, lambda s, up: finish(s))
    each(3, lambda s, up: finish(s))

    for r in range(4):
        for kc in range(r + 1):
            @pl.when((r <= z) & (z < 3))
            def _():
                t_up(r, kc).wait_send()

            @pl.when((r >= z) & (z > 0))
            def _():
                t_dn(r, kc).wait_send()

            t_xn(r, kc).wait_send()
            t_sib(r, kc).wait_send()
            t_fwd(r, kc).wait_send()
        for s in range(4):
            @pl.when((s <= z) & (z < 3) & (z - s < 2))
            def _():
                pz(s, r, True).wait_send()

            @pl.when((s >= z) & (z > 0) & (s - z < 2))
            def _():
                pz(s, r, False).wait_send()

        px(0, c, r).wait_send()
        px(1, c, r).wait_send()
        px(2, xn, r).wait_send()
        for h in (0, 1):
            @pl.when((z == 1) | (z == 2))
            def _():
                ph(3, r, h, False).wait_send()

            if G == 2:
                rs(r, h).wait_send()
            emit(r, h).wait()


def body(G, factor, pivots, constraints):
    nb, piece, order_m = factor.shape
    strip = constraints.shape[2]
    assert strip == W and order_m == 4 * W and piece * 4 == W
    rows_out = 2 * W if G == 2 else 4 * W
    dma = pltpu.SemaphoreType.DMA
    half = (4, 2, 2 * W, W // 2) if G == 2 else (1, 1, 8, 128)
    result = pl.pallas_call(
        functools.partial(kernel, G, nb),
        out_shape=jax.ShapeDtypeStruct((rows_out, 4 * W), f32),
        in_specs=[
            pl.BlockSpec(memory_space=pltpu.VMEM),
            pl.BlockSpec(memory_space=pltpu.VMEM),
            pl.BlockSpec(memory_space=pl.ANY),
        ],
        out_specs=pl.BlockSpec(memory_space=pl.ANY),
        scratch_shapes=[
            pltpu.VMEM((4, nb, 4 * W, W), f32),
            pltpu.VMEM((nb, 4 * W, W), f32),
            pltpu.VMEM((nb, 4 * W, W), bf16),
            pltpu.VMEM((nb, 4 * W, W), bf16),
            pltpu.VMEM((W, W), f32),
            pltpu.VMEM((4, 4, nb * W, W), bf16),
            pltpu.VMEM((4, 4, W, nb * W), bf16),
            pltpu.VMEM((rows_out, 4 * W), f32),
            pltpu.VMEM(half, f32),
            pltpu.VMEM(half, f32),
            dma,
            dma((5, 4, 4)),
            dma((4, 4, 4)),
            dma((2, 4, 4)),
            dma((4, 4)),
            dma((4, 2)),
            dma((4, 2)),
            dma((3, 4)),
            dma((3, 4)),
            dma((4, 2)),
            dma((4, 2)),
            dma((4, 2)),
        ],
        compiler_params=pltpu.CompilerParams(
            collective_id=0, has_side_effects=True, vmem_limit_bytes=52 << 20),
    )(factor, jnp.tile(pivots, (1, 4)), constraints)
    if G != 2:
        result = lax.psum_scatter(result, "grp", scatter_dimension=0, tiled=True)
    return result[None]


def solution(mesh):
    in_specs = (
        P("grp", ("row", "col"), None),
        P("grp", ("row", "col")),
        P("grp", None, ("col", "row")),
    )
    return jax.shard_map(
        functools.partial(body, mesh.shape["grp"]), mesh=mesh, in_specs=in_specs,
        out_specs=P("row", "grp", "col"), check_vma=False)
```
